32 devices in a mesh: tm: 4 (over y, x), space: 8 (over z, core).
Axes of the slice: x: 2, y: 2, z: 4, core: 2. Of those that a mesh axis runs over, the one named last changes fastest.
Arguments:
- ckpt_store: float32 [4, 8, 8, 5120], P('tm', 'space'), may hold values from -6 to 6
- ckpt_target: int32 [4, 8, 8], P('tm'), may hold values from 0 to 7, as said below
- ckpt_block: int32 [4, 8, 8], P('tm'), may hold values from 0 to 7, as said below
- lengths: int32 [4], replicated, may hold values from 1 to 3, 8 in all
- obs_adjoint: float32 [4, 5, 32, 16, 128], P('tm', None, 'space'), may hold values from -6 to 6
- w_in: bfloat16 [16, 135], replicated, may hold values from -0.5 to 0.5
- w_out: bfloat16 [5, 16], replicated, may hold values from -1.5 to 1.5
Outputs:
- start_adjoint: float32 [4, 5, 32, 16, 128], P('tm', None, 'space')
- grad_in: float32 [16, 135], replicated
- grad_out: float32 [5, 16], replicated
The draws below stay inside these ranges and needn't reach their ends.
Inputs may be any that keep to these rules, and one draw needn't show every extreme that they name: In each section every block b of every slab p is stored in exactly one holder and slot, with ckpt_target = p and ckpt_block = b there. One holder stores at most 2 blocks of one slab in a section, and exactly 2 of some. `ckpt_block`: within a section and target slab, the block indices are all different.
All inputs are finite; a program needn't handle non-finite values.
Results may differ from the reference program's by a relative error of at most 0.0083.
Values sent between devices are 32-bit elements; how exact they have to be, the bound alone decides.
A program may use at most 64 MiB of HBM per device.

```python
import math
import jax
import jax.numpy as jnp
import numpy as np
from jax import lax

FIELDS = 5
CHANNELS = 16
CX = 4
NY = 16
NZ = 128
SEC_MOST = 3
NX = 32
BLOCK = 5120
N_TM = 4
N_SPACE = 8


def checkpoint_plan(key):
    slabs = N_SPACE

    def one_section(section_key):
        subkeys = jax.random.split(section_key, 4)
        holders = jax.random.permutation(subkeys[0], slabs).astype(jnp.int32)
        relabel = jax.random.permutation(subkeys[1], slabs).astype(jnp.int32)
        position = jnp.argsort(holders).astype(jnp.int32)
        offsets = jnp.arange(slabs, dtype=jnp.int32)
        base_target = relabel[(position[:, None] + offsets[None, :] // 2) % slabs]
        block_orders = jax.vmap(lambda subkey: jax.random.permutation(subkey, slabs).astype(jnp.int32))(jax.random.split(subkeys[2], slabs))
        base_block = block_orders[base_target, offsets[None, :]]
        slot_orders = jax.vmap(lambda subkey: jax.random.permutation(subkey, slabs).astype(jnp.int32))(jax.random.split(subkeys[3], slabs))
        targets = jnp.take_along_axis(base_target, slot_orders, axis=1)
        blocks = jnp.take_along_axis(base_block, slot_orders, axis=1)
        return (targets.astype(jnp.int32), blocks.astype(jnp.int32))
    section_keys = jax.vmap(lambda section: jax.random.fold_in(key, section))(jnp.arange(N_TM))
    return jax.vmap(one_section)(section_keys)


def draw_ckpt_target(key, part):
    return checkpoint_plan(jax.random.fold_in(key, 7))[0]


def draw_ckpt_block(key, part):
    return checkpoint_plan(jax.random.fold_in(key, 7))[1]


def block_levels(stream_key, shape, cuts, least, largest):
    def one(axis_at, shards_of):
        heights = jax.random.uniform(jax.random.fold_in(jax.random.fold_in(stream_key, 6), axis_at), (shards_of,), jnp.float32, least / len(cuts), largest / len(cuts))
        return jnp.repeat(jnp.exp(heights), shape[axis_at] // shards_of).reshape((-1,) + (1,) * (len(shape) - axis_at - 1))

    factor_of = one(*cuts[0])
    for cut in cuts[1:]:
        factor_of = factor_of * one(*cut)
    return factor_of


def split_up(count, total, bound, skew):
    loads = [(1 << 20) // math.isqrt(standing ** skew) + 1 for standing in range(2, count + 1)]
    spare, counts = total - bound - (count - 1), [1] * (count - 1)
    while spare > 0:
        candidates = [i for i in range(count - 1) if counts[i] < bound]
        whole, left = sum([loads[i] for i in candidates]), spare
        for i in candidates:
            more = min(bound - counts[i], max(1, left * loads[i] // whole), spare)
            counts[i] = counts[i] + more
            spare = spare - more
    return np.array([bound] + counts)


def ragged_sizes(stream_key, amount, total, most, skew):
    if amount == 2:
        one = jax.random.randint(stream_key, (), max(1, total - most), min(most, total - 1) + 1)
        return jnp.stack([one, total - one])
    sizes = jnp.asarray(split_up(amount, total, most, skew), jnp.int32)
    couples = (amount - 1) // 2
    giver, sink = sizes[1:1 + 2 * couples:2], sizes[2:2 + 2 * couples:2]
    margin = jnp.minimum(giver - 1, most - sink)
    passed = jax.random.randint(jax.random.fold_in(stream_key, 1), (couples,), 0, 1 << 20) % (margin + 1)
    sizes = sizes.at[1:1 + 2 * couples:2].set(giver - passed).at[2:2 + 2 * couples:2].set(sink + passed)
    return sizes[jax.random.permutation(jax.random.fold_in(stream_key, 2), amount)]


def centred(rng, shape, width, most, cuts=(), held_as=jnp.bfloat16):
    values = jax.random.normal(rng, shape, jnp.float32) * width
    if len(cuts) > 0:
        values = block_levels(rng, shape, cuts, -0.22, 0.18) * values
    return jnp.clip(values, min=-most, max=most).astype(held_as)


def setup_inputs(seed: int = 0) -> dict:
    splits = jax.random.split(jax.random.key(seed), 8)
    return {
        "ckpt_store": centred(splits[0], (N_TM, N_SPACE, N_SPACE, BLOCK), 1.0, 6.0, ((0, 4), (1, 8)), jnp.float32),
        "ckpt_target": draw_ckpt_target(jax.random.fold_in(splits[7], 71), 0),
        "ckpt_block": draw_ckpt_block(jax.random.fold_in(splits[7], 71), 0),
        "lengths": ragged_sizes(splits[3], N_TM, 2 * N_TM, SEC_MOST, 2).astype(jnp.int32),
        "obs_adjoint": centred(splits[4], (N_TM, FIELDS, NX, NY, NZ), 1.0, 6.0, ((0, 4), (2, 8)), jnp.float32),
        "w_in": centred(splits[5], (CHANNELS, 27 * FIELDS), (27 * FIELDS) ** -0.5, 0.5),
        "w_out": centred(splits[6], (FIELDS, CHANNELS), CHANNELS ** -0.5, 1.5),
    }


TIME_STEP = 0.08
VISCOSITY = 1.0

def physics(padded):
    widened = jnp.pad(padded, ((0, 0), (0, 0), (0, 0), (1, 1)))
    center = widened[:, 1:-1, 1:-1, 1:-1]
    x_plus = widened[:, 2:, 1:-1, 1:-1]
    x_minus = widened[:, :-2, 1:-1, 1:-1]
    y_plus = widened[:, 1:-1, 2:, 1:-1]
    y_minus = widened[:, 1:-1, :-2, 1:-1]
    z_plus = widened[:, 1:-1, 1:-1, 2:]
    z_minus = widened[:, 1:-1, 1:-1, :-2]
    diffuse = x_plus + x_minus + y_plus + y_minus + z_plus + z_minus - 6.0 * center
    carried = center[0:1] * (x_plus - x_minus) * 0.5 + center[1:2] * (y_plus - y_minus) * 0.5 + center[2:3] * (z_plus - z_minus) * 0.5
    return center + TIME_STEP * (VISCOSITY * diffuse - carried)

def gather_taps(padded):
    fields = padded.shape[0]
    planes = padded.shape[1] - 2
    rows_y = padded.shape[2] - 2
    depth = padded.shape[3]
    widened = jnp.pad(padded.astype(jnp.bfloat16), ((0, 0), (0, 0), (0, 0), (1, 1)))
    pieces = []
    for shift_x in range(3):
        for shift_y in range(3):
            for shift_z in range(3):
                pieces.append(widened[:, shift_x:shift_x + planes, shift_y:shift_y + rows_y, shift_z:shift_z + depth])
    return jnp.stack(pieces, 0).reshape(27 * fields, planes * rows_y * depth)

def advance(padded, w_in, w_out):
    flowed = physics(padded)
    taps = gather_taps(padded)
    hidden = jnp.tanh(jnp.dot(w_in, taps, preferred_element_type=jnp.float32))
    learned = jnp.dot(w_out, hidden.astype(jnp.bfloat16), preferred_element_type=jnp.float32)
    return flowed + learned.reshape(flowed.shape)

def retreat(padded, adjoint, w_in, w_out):
    fields = padded.shape[0]
    planes = padded.shape[1] - 2
    rows_y = padded.shape[2] - 2
    depth = padded.shape[3]
    _, pull_back = jax.vjp(physics, padded)
    through_flow, = pull_back(adjoint)
    taps = gather_taps(padded)
    hidden = jnp.tanh(jnp.dot(w_in, taps, preferred_element_type=jnp.float32))
    hidden_low = hidden.astype(jnp.bfloat16)
    adjoint_low = adjoint.reshape(fields, planes * rows_y * depth).astype(jnp.bfloat16)
    contract = (((1,), (1,)), ((), ()))
    part_out = lax.dot_general(adjoint_low, hidden_low, contract, preferred_element_type=jnp.float32)
    back_hidden = jnp.dot(w_out.T, adjoint_low, preferred_element_type=jnp.float32) * (1.0 - hidden * hidden)
    back_low = back_hidden.astype(jnp.bfloat16)
    part_in = lax.dot_general(back_low, taps, contract, preferred_element_type=jnp.float32)
    back_taps = jnp.dot(w_in.T, back_low, preferred_element_type=jnp.float32).reshape(27, fields, planes, rows_y, depth)
    spread_sum = None
    for shift_x in range(3):
        for shift_y in range(3):
            for shift_z in range(3):
                tap_index = 9 * shift_x + 3 * shift_y + shift_z
                placed = jnp.pad(back_taps[tap_index], ((0, 0), (shift_x, 2 - shift_x), (shift_y, 2 - shift_y), (shift_z, 2 - shift_z)))
                spread_sum = placed if spread_sum is None else spread_sum + placed
    return (through_flow + spread_sum[:, :, :, 1:-1], part_in, part_out)

def reference(ckpt_store, ckpt_target, ckpt_block, lengths, obs_adjoint, w_in, w_out):
    slabs = ckpt_store.shape[1]
    block_size = ckpt_store.shape[3]
    fields = obs_adjoint.shape[1]
    adjoint = jnp.zeros(obs_adjoint.shape[1:], jnp.float32)
    grad_in = jnp.zeros(w_in.shape, jnp.float32)
    grad_out = jnp.zeros(w_out.shape, jnp.float32)
    results = []
    for section in reversed(range(N_TM)):
        pieces = jnp.zeros((slabs, slabs, block_size), jnp.float32)
        pieces = pieces.at[ckpt_target[section], ckpt_block[section]].set(ckpt_store[section])
        state = pieces.reshape(slabs, fields, CX, NY, NZ).transpose(1, 0, 2, 3, 4).reshape(fields, NX, NY, NZ)
        step_count = lengths[section]
        stored = []
        for position in range(SEC_MOST):
            padded = jnp.pad(state, ((0, 0), (1, 1), (1, 1), (0, 0)))
            stored.append(padded)
            state = jnp.where(position < step_count, advance(padded, w_in, w_out), state)
        adjoint = obs_adjoint[section] + adjoint
        for position in reversed(range(SEC_MOST)):
            pulled, part_in, part_out = retreat(stored[position], adjoint, w_in, w_out)
            live = position < step_count
            adjoint = jnp.where(live, pulled[:, 1:-1, 1:-1, :], adjoint)
            grad_in = grad_in + jnp.where(live, part_in, 0.0)
            grad_out = grad_out + jnp.where(live, part_out, 0.0)
        results.append(adjoint)
    start_adjoint = jnp.stack(results[::-1], 0)
    scale = 1.0 / math.sqrt(NX * NY * NZ)
    return (start_adjoint, grad_in * scale, grad_out * scale)
```

```python
import functools
import math

import jax
import jax.numpy as jnp
from jax import lax
from jax.experimental import pallas as pl
from jax.experimental.pallas import tpu as pltpu
from jax.sharding import PartitionSpec as P

SEC_MOST = 3
DT = 0.08
MESH = pl.DeviceIdType.MESH
F32 = jnp.float32
BF16 = jnp.bfloat16


def table_kernel(slabs, targets_ref, blocks_ref, table_ref):
    me = lax.axis_index("space")

    def holder(h, _):
        def slot(j, count):
            mine = targets_ref[h, j] == me

            @pl.when(mine)
            def _():
                table_ref[blocks_ref[h, j]] = 2 * h + count

            return count + jnp.where(mine, 1, 0)

        lax.fori_loop(0, slabs, slot, 0)
        return 0

    lax.fori_loop(0, slabs, holder, 0)


def picks(shape, axis, middle, last, fields):
    j = lax.broadcasted_iota(jnp.int32, shape, axis)
    i = lax.broadcasted_iota(jnp.int32, shape, 1 - axis)
    outer = jnp.where(j >= 24, 1, 0) + jnp.where(j >= 48, 1, 0)
    inner = (j >> 3) - 3 * outer
    f = j & 7
    source = (9 * outer + middle * inner + last) * fields + f
    return jnp.logical_and(jnp.logical_and(f < fields, j < 72), i == source)


def finish_kernel(state_ref, sums_ref, out_ref, gin_ref, gout_ref):
    planes, ny, fields = state_ref.shape[:3]
    for q in range(planes):
        for y in range(ny):
            for f in range(fields):
                out_ref[f, q, y : y + 1, :] = state_ref[q, y, f : f + 1, :]
    taps_all = gin_ref.shape[1]
    total_in = jnp.zeros((16, taps_all), F32)
    for c in range(3):
        sel = jnp.where(picks((80, taps_all), 0, 3, c, fields), 1.0, 0.0)
        total_in = total_in + jnp.dot(
            sums_ref[16 * c : 16 * c + 16, 0:80], sel, precision=lax.Precision.HIGHEST,
            preferred_element_type=F32,
        )
    gin_ref[...] = total_in
    gout_ref[...] = sums_ref[48 : 48 + fields, 0:16]


def main_kernel(
    dims,
    store, targets, blocks, given, lengths, obs_in, w_in, w_out,
    out_ref, gfin,
    outgoing, obs, table,
    arrived, full, stc, obsr, taps, dh, hl, pd, gl, blp, own, hist, sendp, sendm, recvp, recvm,
    osend, u_ref, c_ref, wf, wc, wo, wot, pin_ref, pout_ref, gpart, g1, g2, g3,
    a2a_s, a2a_r, init_s, init_r, obs_s, obs_r, fwd_s, fwd_r, ch_s, ch_r, out_s, out_r, loc, r1_s, r1_r, r2_s, r2_r, r3_s, r3_r, pair_s, pair_r,
):
    sections, slabs, planes, ny, fields, rows, steps, scale = dims
    t = lax.axis_index("tm")
    p = lax.axis_index("space")
    nx = slabs * planes

    def gray(r):
        return r + (r // 2) * (1 - 2 * (r % 2))

    def flip(pp, i):
        return i + (pp % 2) * (planes - 1 - 2 * i)

    def device_of(x):
        pair = x // (2 * planes)
        i = x % (2 * planes)
        return gray(flip(pair, i // 2)), 2 * pair + i % 2

    active = t < planes
    x = (p // 2) * 2 * planes + 2 * flip(p // 2, gray(t)) + p % 2
    home, spot = x // planes, x % planes

    def rcopy(src, dst, ss, rs, tt, pp):
        return pltpu.make_async_remote_copy(
            src_ref=src, dst_ref=dst, send_sem=ss, recv_sem=rs,
            device_id={"tm": tt, "space": pp}, device_id_type=MESH,
        )

    barrier = pltpu.get_barrier_semaphore()

    def hello(there, slab):
        pl.semaphore_signal(
            barrier, inc=1, device_id={"tm": there, "space": slab}, device_id_type=MESH
        )

    def greet(j, _):
        hello(t, (p + j) % slabs)
        return 0

    if slabs <= 16:
        for j in range(1, slabs):
            greet(j, 0)
    else:
        lax.fori_loop(1, slabs, greet, 0)
    for gap in (-1, 0, 1):
        layer = p // 2 + gap

        @pl.when(jnp.logical_and(layer >= 0, layer < slabs // 2))
        def _():
            for j in range(1, sections):
                for c in range(2):
                    hello((t + j) % sections, 2 * layer + c)

    def group(q, _):
        def slot(j, found):
            count, one, two = found
            hit = targets[p, j] == q
            one = jnp.where(jnp.logical_and(hit, count == 0), j, one)
            two = jnp.where(jnp.logical_and(hit, count == 1), j, two)
            return count + jnp.where(hit, 1, 0), one, two

        zero = jnp.int32(0)
        if slabs <= 16:
            found = (zero, zero, zero)
            for j in range(slabs):
                found = slot(j, found)
        else:
            found = lax.fori_loop(0, slabs, slot, (zero, zero, zero))
        for rank in range(2):
            line = store[pl.ds(found[1 + rank], 1), :]
            for k in range(rows):
                outgoing[q, rank, pl.ds(k, 1), :] = line[:, k * 128 : (k + 1) * 128]
        return 0

    lax.fori_loop(0, slabs, group, 0)
    for q in range(planes):
        for y in range(ny):
            for f in range(fields):
                obs[q, y, f : f + 1, :] = obs_in[f, q, y : y + 1, :]
    beside = 1 + jnp.where(p // 2 > 0, 1, 0) + jnp.where(p // 2 < slabs // 2 - 1, 1, 0)
    pl.semaphore_wait(barrier, slabs - 1 + (sections - 1) * 2 * beside)

    def a2a(peer):
        return rcopy(outgoing.at[peer], arrived.at[p], a2a_s.at[peer], a2a_r.at[p], t, peer)

    def a2a_start(j, _):
        far = slabs - j

        @pl.when(p + far < slabs)
        def _():
            a2a(p + far).start()

        @pl.when(p >= far)
        def _():
            a2a(p - far).start()

        return 0

    lax.fori_loop(1, slabs, a2a_start, 0)
    keep = pltpu.make_async_copy(outgoing.at[p], arrived.at[p], loc.at[0])
    keep.start()

    def each_obs(q, action):
        tt, pp = device_of(p * planes + q)
        same = jnp.logical_and(tt == t, pp == p)

        @pl.when(jnp.logical_not(same))
        def _():
            action(rcopy(obs.at[q], obsr.at[t], obs_s.at[q], obs_r.at[t], tt, pp), False)

        @pl.when(same)
        def _():
            action(pltpu.make_async_copy(obs.at[q], obsr.at[t], loc.at[1]), True)

    for q in range(planes):
        each_obs(q, lambda c, same: c.start())

    zeros5 = jnp.zeros((fields, 128), F32)

    taps_all = w_in.shape[1]
    weights = w_in[...]
    nt = (((1,), (1,)), ((), ()))
    for c in range(3):
        sel = jnp.where(picks((taps_all, 80), 1, 3, c, fields), 1.0, 0.0).astype(BF16)
        wf[16 * c : 16 * c + 16, :] = jnp.dot(weights, sel, preferred_element_type=F32).astype(BF16)
    for b in range(3):
        sel = jnp.where(picks((72, taps_all), 0, 1, 3 * b, fields), 1.0, 0.0).astype(BF16)
        wc[:, 16 * b : 16 * b + 16] = lax.dot_general(
            sel, weights, nt, preferred_element_type=F32
        ).astype(BF16)
    wide_out = jnp.concatenate(
        [w_out[...].astype(F32), jnp.zeros((16 - fields, 16), F32)], axis=0
    ).astype(BF16)
    wo[...] = wide_out
    eye = jnp.where(
        lax.broadcasted_iota(jnp.int32, (16, 16), 0) == lax.broadcasted_iota(jnp.int32, (16, 16), 1),
        1.0, 0.0,
    ).astype(BF16)
    wot[...] = lax.dot_general(eye, wide_out, nt, preferred_element_type=F32).astype(BF16)
    pin_ref[...] = jnp.zeros(pin_ref.shape, F32)
    pout_ref[...] = jnp.zeros(pout_ref.shape, F32)
    gpart[...] = jnp.zeros(gpart.shape, F32)

    def place(b, _):
        def holder(h, found):
            count = jnp.int32(0)
            for j in range(slabs):
                hit = targets[h, j] == p
                at = jnp.logical_and(hit, blocks[h, j] == b)
                found = jnp.where(at, 2 * h + count, found)
                count = count + jnp.where(hit, 1, 0)
            return found

        table[b] = lax.fori_loop(0, slabs, holder, jnp.int32(0))
        return 0

    if slabs <= 16:
        lax.fori_loop(0, slabs, place, 0)

    def blank(slot, recv):
        def one(i, _):
            for n in range(SEC_MOST):
                for y in range(ny):
                    stc[n, i, slot, y] = zeros5
            return 0

        lax.fori_loop(0, sections, one, 0)

        def two(i, _):
            for y in range(ny):
                recv[i, y] = zeros5
            return 0

        lax.fori_loop(0, steps, two, 0)

    @pl.when(jnp.logical_and(active, x == 0))
    def _():
        blank(0, recvm)

    @pl.when(jnp.logical_and(active, x == nx - 1))
    def _():
        blank(2, recvp)

    def a2a_wait(j, _):
        peer = (p + j) % slabs
        rcopy(outgoing.at[p], arrived.at[peer], a2a_s.at[peer], a2a_r.at[peer], t, peer).wait()
        return 0

    lax.fori_loop(1, slabs, a2a_wait, 0)
    keep.wait()

    for b in range(slabs):
        where = jnp.clip((table if slabs <= 16 else given)[b], 0, 2 * slabs - 1)
        holder = where // 2
        rank = where % 2
        for k in range(rows):
            r = b * rows + k
            f, rest = divmod(r, planes * ny)
            xx, y = divmod(rest, ny)
            full[xx, y, pl.ds(f, 1), :] = arrived[holder, rank, pl.ds(k, 1), :]

    def each_init(q, j, action):
        if (q % 2, j) in ((0, 0), (1, 2)):
            return
        xd = p * planes + q + 1 - j

        @pl.when(jnp.logical_and(xd >= 0, xd < nx))
        def _():
            tt, pp = device_of(xd)
            same = jnp.logical_and(tt == t, pp == p)

            @pl.when(jnp.logical_not(same))
            def _():
                action(
                    rcopy(full.at[q], stc.at[0, t, j], init_s.at[q, j], init_r.at[t, j], tt, pp),
                    False,
                )

            @pl.when(same)
            def _():
                action(pltpu.make_async_copy(full.at[q], stc.at[0, t, j], loc.at[2 + j]), True)

    for j in (1, 0, 2):
        for q in range(planes):
            each_init(q, j, lambda c, same: c.start())

    def finish(c, same):
        if same:
            c.wait()
        else:
            c.wait_send()

    lane = lax.broadcasted_iota(jnp.int32, (16, 128), 1)

    def up(v):
        return jnp.where(lane[: v.shape[0]] == 0, 0.0, pltpu.roll(v, 1, 1))

    def down(v):
        return jnp.where(lane[: v.shape[0]] == 127, 0.0, pltpu.roll(v, 127, 1))

    zeros3 = jnp.zeros((8 - fields, 128), F32)
    zeros8 = jnp.zeros((8, 128), F32)

    def pad8(v):
        return jnp.concatenate([v, zeros3], axis=0)

    def lanes(y):
        return slice(y * 128, (y + 1) * 128)

    t_next, p_next = device_of(x + 1)
    t_prev, p_prev = device_of(x + nx - 1 - nx * jnp.where(x > 0, 1, 0))

    def fwd(n, s, way):
        if way == 0:
            return rcopy(stc.at[n, s, 1], stc.at[n, s, 0], fwd_s.at[n - 1, s, 0],
                         fwd_r.at[n - 1, s, 0], t_next, p_next)
        return rcopy(stc.at[n, s, 1], stc.at[n, s, 2], fwd_s.at[n - 1, s, 1],
                     fwd_r.at[n - 1, s, 1], t_prev, p_prev)

    def both(make, action_next, action_prev):
        @pl.when(x < nx - 1)
        def _():
            action_next(make)

        @pl.when(x > 0)
        def _():
            action_prev(make)

    outer = 2 * (p % 2)
    partner = 2 * (p // 2) + 1 - p % 2

    def init_wait(s, j):
        xs = x - 1 + j
        ok = jnp.logical_and(xs >= 0, xs < nx)
        local_one = jnp.logical_and(s == t, (xs + planes) // planes - 1 == p)

        @pl.when(jnp.logical_and(ok, jnp.logical_not(local_one)))
        def _():
            rcopy(full.at[0], stc.at[0, s, j], init_s.at[0, 1], init_r.at[s, j], t, p).wait_recv()

        @pl.when(jnp.logical_and(ok, local_one))
        def _():
            pltpu.make_async_copy(full.at[0], stc.at[0, s, j], loc.at[2 + j]).wait()

    def pass_on(s):
        return rcopy(stc.at[0, s, 1], stc.at[0, s, outer], pair_s.at[s], pair_r.at[s], t, partner)

    def pass_in(s):
        return rcopy(stc.at[0, s, 1], stc.at[0, s, 2 - outer], pair_s.at[s], pair_r.at[s], t, partner)

    def forward(n, s):
        if n == 0:
            init_wait(s, outer)
            pass_in(s).wait_recv()
        else:
            @pl.when(x > 0)
            def _():
                fwd(n, s, 0).wait_recv()

            @pl.when(x < nx - 1)
            def _():
                fwd(n, s, 1).wait_recv()

        def row(a, y):
            if y < 0 or y >= ny:
                return zeros8
            return pad8(stc[n, s, a, y])

        for y in range(ny):
            parts = [row(a, y + b) for a in range(3) for b in (-1, 0, 1)] + [zeros8]
            taps[n, s, :, lanes(y)] = jnp.concatenate(parts, axis=0).astype(BF16)
        u_ref[0:48, :] = jnp.dot(wf[...], taps[n, s], preferred_element_type=F32)
        for y in range(ny):
            u = u_ref[16:32, lanes(y)] + up(u_ref[0:16, lanes(y)]) + down(u_ref[32:48, lanes(y)])
            h = jnp.tanh(u)
            hl[n, s, :, lanes(y)] = h.astype(BF16)
            dh[n, s, :, lanes(y)] = 1.0 - h * h
        last = n == SEC_MOST - 1
        if not last:
            c_ref[0:16, :] = jnp.dot(wo[...], hl[n, s], preferred_element_type=F32)
        for y in range(ny):
            v = row(1, y)
            xm, xp, ym, yp = row(0, y), row(2, y), row(1, y - 1), row(1, y + 1)
            zm, zp = up(v), down(v)
            dx, dy, dz = (xp - xm) * 0.5, (yp - ym) * 0.5, (zp - zm) * 0.5
            pd[n, s, y, 0] = dx * DT
            pd[n, s, y, 1] = dy * DT
            pd[n, s, y, 2] = dz * DT
            pd[n, s, y, 3] = v
            if not last:
                lap = xp + xm + yp + ym + zp + zm - 6.0 * v
                adv = v[0:1] * dx + v[1:2] * dy + v[2:3] * dz
                new = v + DT * (lap - adv) + c_ref[0:8, lanes(y)]
                stc[n + 1, s, 1, y] = new[:fields]
        if not last:
            @pl.when(x < nx - 1)
            def _():
                fwd(n + 1, s, 0).start()

            @pl.when(x > 0)
            def _():
                fwd(n + 1, s, 1).start()

    sub = lax.broadcasted_iota(jnp.int32, (8, 128), 0)

    crew = 2 * sections
    bands = slabs // 2
    part = 64 // crew
    seat = 2 * t + p % 2

    def mate(j):
        i = (seat + j) % crew
        return i, i // 2, 2 * (p // 2) + i % 2

    def red1(j):
        i, tt, pp = mate(j)
        return rcopy(gpart.at[i], g1.at[seat], r1_s.at[i], r1_r.at[seat], tt, pp)

    def red1_in(j):
        i, tt, pp = mate(j)
        return rcopy(gpart.at[i], g1.at[i], r1_s.at[i], r1_r.at[i], tt, pp)

    def red2(j):
        i = (p // 2 + j) % bands
        return rcopy(g2, g3.at[p // 2], r2_s.at[i], r2_r.at[p // 2], t, 2 * i + p % 2)

    def red2_in(j):
        i = (p // 2 + j) % bands
        return rcopy(g2, g3.at[i], r2_s.at[i], r2_r.at[i], t, 2 * i + p % 2)

    def red3(j):
        i, tt, pp = mate(j)
        return rcopy(gfin.at[seat], gfin.at[seat], r3_s.at[i], r3_r.at[seat], tt, pp)

    def red3_in(j):
        i, tt, pp = mate(j)
        return rcopy(gfin.at[i], gfin.at[i], r3_s.at[i], r3_r.at[i], tt, pp)

    def band_loop(make, action):
        def one(j, _):
            action(make(j))
            return 0

        lax.fori_loop(1, bands, one, 0)

    def red1_begin():
        for r in range(0, 64, part):
            if r < 48:
                gpart[r // part, :, 0:80] = pin_ref[r : r + part, :]
            else:
                gpart[r // part, :, 0:16] = pout_ref[r - 48 : r - 48 + part, :]
        for j in range(1, crew):
            red1(j).start()
        g1[seat] = gpart[seat]

    def chain(way, k):
        if way == 0:
            return rcopy(sendp.at[k], recvm.at[k], ch_s.at[k, 0], ch_r.at[k, 0], t_next, p_next)
        return rcopy(sendm.at[k], recvp.at[k], ch_s.at[k, 1], ch_r.at[k, 1], t_prev, p_prev)

    @pl.when(active)
    def _():
        def relay(i, _):
            s = sections - 1 - i
            init_wait(s, 1)
            pass_on(s).start()
            return 0

        lax.fori_loop(0, sections, relay, 0)
        for n in range(SEC_MOST):
            def turn(i, _):
                forward(n, sections - 1 - i)
                return 0

            lax.fori_loop(0, sections, turn, 0)

        def obs_wait(s, _):
            same = jnp.logical_and(s == t, home == p)

            @pl.when(jnp.logical_not(same))
            def _():
                rcopy(obs.at[0], obsr.at[s], obs_s.at[0], obs_r.at[s], t, p).wait_recv()

            @pl.when(same)
            def _():
                pltpu.make_async_copy(obs.at[0], obsr.at[s], loc.at[1]).wait()

            return 0

        lax.fori_loop(0, sections, obs_wait, 0)

        blp[:, 0:128] = jnp.zeros((16, 128), BF16)
        blp[:, (ny + 1) * 128 :] = jnp.zeros((16, 128), BF16)
        for y in range(ny):
            hist[0, y] = zeros8

        size = [lengths[s] for s in range(sections)]
        after = [None] * sections
        run = jnp.int32(0)
        for s in reversed(range(sections)):
            after[s] = run
            run = run + size[s]

        def step(k, _):
            s = jnp.int32(0)
            for i in range(sections - 1):
                s = s + jnp.where(after[i] > k, 1, 0)
            n = jnp.int32(0)
            begin = jnp.int32(0)
            for i in range(sections):
                n = n + jnp.where(s == i, after[i] + size[i] - 1 - k, 0)
                begin = begin + jnp.where(s == i, after[i], 0)
            n = jnp.clip(n, 0, SEC_MOST - 1)
            first = begin == k
            weight = jnp.where(first, 1.0, 0.0).astype(F32)

            g = []
            for y in range(ny):
                v = hist[k, y] + pad8(obsr[s, y]) * weight
                g.append(v)
                gl[:, lanes(y)] = jnp.concatenate([v, zeros8], axis=0).astype(BF16)
            b32 = jnp.dot(wot[...], gl[...], preferred_element_type=F32) * dh[n, s]
            blp[:, 128 : (ny + 1) * 128] = b32.astype(BF16)
            wide = ny * 128
            stack = jnp.concatenate(
                [blp[:, 256 : 256 + wide], blp[:, 128 : 128 + wide], blp[:, 0:wide]], axis=0
            )
            c_ref[0:24, :] = jnp.dot(wc[0:24, :], stack, preferred_element_type=F32)
            c_ref[48:72, :] = jnp.dot(wc[48:72, :], stack, preferred_element_type=F32)

            def conv(a, c, y):
                return c_ref[(3 * a + c) * 8 : (3 * a + c + 1) * 8, lanes(y)]

            def speed(d, y):
                return pd[n, s, y, 3, pl.ds(d, 1), :]

            for y in range(ny):
                even = g[y] * DT
                m0 = g[y] * (0.5 * DT) * speed(0, y)
                to_next = even - m0 + conv(2, 1, y) + down(conv(2, 0, y)) + up(conv(2, 2, y))
                to_prev = even + m0 + conv(0, 1, y) + down(conv(0, 0, y)) + up(conv(0, 2, y))
                sendp[k, y] = to_next[:fields]
                sendm[k, y] = to_prev[:fields]

            @pl.when(x < nx - 1)
            def _():
                chain(0, k).start()

            @pl.when(x > 0)
            def _():
                chain(1, k).start()

            base = blp[:, 128 : 128 + wide]
            for y in range(ny):
                r = blp[:, 128 + y * 128 : 256 + y * 128].astype(F32)
                u_ref[0:16, lanes(y)] = down(r)
                u_ref[16:32, lanes(y)] = up(r)
            grads = jnp.concatenate(
                [u_ref[0:16, :].astype(BF16), base, u_ref[16:32, :].astype(BF16)], axis=0
            )
            pin_ref[...] += lax.dot_general(grads, taps[n, s], nt, preferred_element_type=F32)
            pout_ref[...] += lax.dot_general(gl[...], hl[n, s], nt, preferred_element_type=F32)

            @pl.when(k == steps - 1)
            def _():
                red1_begin()

            c_ref[24:48, :] = jnp.dot(wc[24:48, :], stack, preferred_element_type=F32)
            push, pull = [], []
            for y in range(ny):
                half = g[y] * (0.5 * DT)
                even = g[y] * DT
                m1, m2 = half * speed(1, y), half * speed(2, y)
                push.append(even - m1)
                pull.append(even + m1)
                here = g[y] * (1.0 - 6.0 * DT) + conv(1, 1, y)
                here = here + up(even - m2 + conv(1, 2, y)) + down(even + m2 + conv(1, 0, y))
                for d in range(3):
                    term = jnp.sum(g[y] * pd[n, s, y, d], axis=0, keepdims=True)
                    here = here - jnp.where(sub == d, term, 0.0)
                own[y] = here

            for y in range(ny):
                add = own[y]
                if y > 0:
                    add = add + push[y - 1]
                if y < ny - 1:
                    add = add + pull[y + 1]
                own[y] = add

            @pl.when(x > 0)
            def _():
                chain(0, k).wait_recv()

            @pl.when(x < nx - 1)
            def _():
                chain(1, k).wait_recv()

            for y in range(ny):
                hist[k + 1, y] = own[y] + pad8(recvm[k, y]) + pad8(recvp[k, y])
            return 0

        lax.fori_loop(0, steps, step, 0)

        for s in range(sections):
            at = jnp.clip(after[s] + size[s], 0, steps)
            for y in range(ny):
                osend[s, y] = hist[at, y][:fields]
        for s in range(sections):
            same = jnp.logical_and(s == t, home == p)

            @pl.when(jnp.logical_not(same))
            def _():
                rcopy(osend.at[s], out_ref.at[spot], out_s.at[s], out_r.at[spot], s, home).start()

            @pl.when(same)
            def _():
                pltpu.make_async_copy(osend.at[s], out_ref.at[spot], loc.at[5]).start()

    @pl.when(jnp.logical_not(active))
    def _():
        red1_begin()

    for j in range(1, crew):
        red1_in(j).wait()
    run1 = g1[0]
    for q in range(1, crew):
        run1 = run1 + g1[q]
    g2[...] = run1
    band_loop(red2, lambda c: c.start())
    g3[p // 2] = run1
    band_loop(red2_in, lambda c: c.wait())
    run2 = g3[0]
    for q in range(1, bands):
        run2 = run2 + g3[q]
    gfin[seat] = run2 * scale
    for j in range(1, crew):
        red3(j).start()

    for q in range(planes):
        tt, pp = device_of(p * planes + q)
        same = jnp.logical_and(tt == t, pp == p)

        @pl.when(jnp.logical_not(same))
        def _():
            rcopy(osend.at[0], out_ref.at[q], out_s.at[0], out_r.at[q], tt, pp).wait_recv()

        @pl.when(same)
        def _():
            pltpu.make_async_copy(osend.at[0], out_ref.at[q], loc.at[5]).wait()

    for q in range(planes):
        each_obs(q, lambda c, same: None if same else c.wait_send())
        for j in range(3):
            each_init(q, j, lambda c, same: None if same else c.wait_send())

    @pl.when(active)
    def _():
        def sent(s, _):
            @pl.when(jnp.logical_not(jnp.logical_and(s == t, home == p)))
            def _():
                rcopy(osend.at[s], out_ref.at[spot], out_s.at[s], out_r.at[spot], s, home).wait_send()

            pass_on(s).wait_send()
            for n in range(1, SEC_MOST):
                @pl.when(x < nx - 1)
                def _():
                    fwd(n, s, 0).wait_send()

                @pl.when(x > 0)
                def _():
                    fwd(n, s, 1).wait_send()

            return 0

        lax.fori_loop(0, sections, sent, 0)

        def sent_chain(k, _):
            @pl.when(x < nx - 1)
            def _():
                chain(0, k).wait_send()

            @pl.when(x > 0)
            def _():
                chain(1, k).wait_send()

            return 0

        lax.fori_loop(0, steps, sent_chain, 0)

    for j in range(1, crew):
        red3_in(j).wait()


def local(ckpt_store, ckpt_target, ckpt_block, lengths, obs_adjoint, w_in, w_out):
    slabs = lax.axis_size("space")
    sections = lax.axis_size("tm")
    observed = obs_adjoint[0]
    fields, planes, ny, depth = observed.shape
    block = ckpt_store.shape[3]
    rows = block // depth
    steps = 2 * sections
    channels = w_in.shape[0]
    grad_scale = 1.0 / math.sqrt(planes * slabs * ny * depth)
    vmem = pl.BlockSpec(memory_space=pltpu.VMEM)
    smem = pl.BlockSpec(memory_space=pltpu.SMEM)

    given = lengths
    if slabs > 16:
        given = pl.pallas_call(
            functools.partial(table_kernel, slabs),
            out_shape=jax.ShapeDtypeStruct((slabs,), jnp.int32),
            in_specs=[smem, smem],
            out_specs=smem,
            name="table",
        )(ckpt_target[0], ckpt_block[0])
    dims = (sections, slabs, planes, ny, fields, rows, steps, grad_scale)
    crew = 2 * sections
    part = 64 // crew
    wide = ny * depth
    face = (ny, fields, depth)
    dma = pltpu.SemaphoreType.DMA
    out, sums = pl.pallas_call(
        functools.partial(main_kernel, dims),
        out_shape=(
            jax.ShapeDtypeStruct((planes,) + face, F32),
            jax.ShapeDtypeStruct((crew, part, depth), F32),
        ),
        in_specs=[vmem, smem, smem, smem, smem, vmem, vmem, vmem],
        out_specs=(vmem, vmem),
        scratch_shapes=[
            pltpu.VMEM((slabs, 2, rows, depth), F32),
            pltpu.VMEM((planes,) + face, F32),
            pltpu.SMEM((slabs,), jnp.int32),
            pltpu.VMEM((slabs, 2, rows, depth), F32),
            pltpu.VMEM((planes,) + face, F32),
            pltpu.VMEM((SEC_MOST, sections, 3) + face, F32),
            pltpu.VMEM((sections,) + face, F32),
            pltpu.VMEM((SEC_MOST, sections, 80, wide), BF16),
            pltpu.VMEM((SEC_MOST, sections, 16, wide), F32),
            pltpu.VMEM((SEC_MOST, sections, 16, wide), BF16),
            pltpu.VMEM((SEC_MOST, sections, ny, 4, 8, depth), F32),
            pltpu.VMEM((16, wide), BF16),
            pltpu.VMEM((16, wide + 2 * depth), BF16),
            pltpu.VMEM((ny, 8, depth), F32),
            pltpu.VMEM((steps + 1, ny, 8, depth), F32),
            pltpu.VMEM((steps,) + face, F32),
            pltpu.VMEM((steps,) + face, F32),
            pltpu.VMEM((steps,) + face, F32),
            pltpu.VMEM((steps,) + face, F32),
            pltpu.VMEM((sections,) + face, F32),
            pltpu.VMEM((64, wide), F32),
            pltpu.VMEM((72, wide), F32),
            pltpu.VMEM((48, 80), BF16),
            pltpu.VMEM((72, 48), BF16),
            pltpu.VMEM((16, 16), BF16),
            pltpu.VMEM((16, 16), BF16),
            pltpu.VMEM((48, 80), F32),
            pltpu.VMEM((16, 16), F32),
            pltpu.VMEM((crew, part, depth), F32),
            pltpu.VMEM((crew, part, depth), F32),
            pltpu.VMEM((part, depth), F32),
            pltpu.VMEM((slabs // 2, part, depth), F32),
            dma((slabs,)), dma((slabs,)),
            dma((planes, 3)), dma((sections, 3)),
            dma((planes,)), dma((sections,)),
            dma((SEC_MOST - 1, sections, 2)), dma((SEC_MOST - 1, sections, 2)),
            dma((steps, 2)), dma((steps, 2)),
            dma((sections,)), dma((planes,)),
            dma((6,)),
            dma((crew,)), dma((crew,)),
            dma((slabs // 2,)), dma((slabs // 2,)),
            dma((crew,)), dma((crew,)),
            dma((sections,)), dma((sections,)),
        ],
        compiler_params=pltpu.CompilerParams(
            collective_id=0, has_side_effects=True, vmem_limit_bytes=56 * 1024 * 1024
        ),
        name="main",
    )(ckpt_store[0, 0], ckpt_target[0], ckpt_block[0], given, lengths, observed, w_in, w_out)

    start_adjoint, grad_in, grad_out = pl.pallas_call(
        finish_kernel,
        out_shape=(
            jax.ShapeDtypeStruct(observed.shape, F32),
            jax.ShapeDtypeStruct(w_in.shape, F32),
            jax.ShapeDtypeStruct(w_out.shape, F32),
        ),
        in_specs=[vmem, vmem],
        out_specs=(vmem, vmem, vmem),
        name="finish",
    )(out, sums.reshape(64, depth))
    return (start_adjoint[None], grad_in, grad_out)


def solution(mesh):
    placed = (
        P("tm", "space", None, None),
        P("tm", None, None),
        P("tm", None, None),
        P(),
        P("tm", None, "space", None, None),
        P(),
        P(),
    )
    return jax.shard_map(
        local,
        mesh=mesh,
        in_specs=placed,
        out_specs=(P("tm", None, "space", None, None), P(), P()),
        check_vma=False,
    )
```

```python
import functools
import math

import jax
import jax.numpy as jnp
from jax import lax
from jax.experimental import pallas as pl
from jax.experimental.pallas import tpu as pltpu
from jax.sharding import PartitionSpec as P

SEC_MOST = 3
DT = 0.08
MESH = pl.DeviceIdType.MESH
F32 = jnp.float32
BF16 = jnp.bfloat16


def table_kernel(slabs, targets_ref, blocks_ref, table_ref):
    me = lax.axis_index("space")

    def holder(h, _):
        def slot(j, count):
            mine = targets_ref[h, j] == me

            @pl.when(mine)
            def _():
                table_ref[blocks_ref[h, j]] = 2 * h + count

            return count + jnp.where(mine, 1, 0)

        lax.fori_loop(0, slabs, slot, 0)
        return 0

    lax.fori_loop(0, slabs, holder, 0)


def picks(shape, axis, middle, last, fields):
    j = lax.broadcasted_iota(jnp.int32, shape, axis)
    i = lax.broadcasted_iota(jnp.int32, shape, 1 - axis)
    outer = jnp.where(j >= 24, 1, 0) + jnp.where(j >= 48, 1, 0)
    inner = (j >> 3) - 3 * outer
    f = j & 7
    source = (9 * outer + middle * inner + last) * fields + f
    return jnp.logical_and(jnp.logical_and(f < fields, j < 72), i == source)


def finish_kernel(state_ref, sums_ref, out_ref, gin_ref, gout_ref):
    planes, ny, fields = state_ref.shape[:3]
    for q in range(planes):
        for y in range(ny):
            for f in range(fields):
                out_ref[f, q, y : y + 1, :] = state_ref[q, y, f : f + 1, :]
    taps_all = gin_ref.shape[1]
    total_in = jnp.zeros((16, taps_all), F32)
    for c in range(3):
        sel = jnp.where(picks((80, taps_all), 0, 3, c, fields), 1.0, 0.0)
        total_in = total_in + jnp.dot(
            sums_ref[16 * c : 16 * c + 16, 0:80], sel, precision=lax.Precision.HIGHEST,
            preferred_element_type=F32,
        )
    gin_ref[...] = total_in
    gout_ref[...] = sums_ref[48 : 48 + fields, 0:16]


def main_kernel(
    dims,
    store, targets, blocks, given, lengths, obs_in, w_in, w_out,
    out_ref, gfin,
    outgoing, obs, table,
    arrived, full, stc, obsr, taps, dh, hl, pd, gl, blp, own, hist, sendp, sendm, recvp, recvm,
    osend, u_ref, c_ref, wf, wc, wo, wot, pin_ref, pout_ref, gpart, g1, g2, g3,
    a2a_s, a2a_r, init_s, init_r, obs_s, obs_r, fwd_s, fwd_r, ch_s, ch_r, out_s, out_r, loc, r1_s, r1_r, r2_s, r2_r, r3_s, r3_r, pair_s, pair_r,
):
    sections, slabs, planes, ny, fields, rows, steps, scale = dims
    t = lax.axis_index("tm")
    p = lax.axis_index("space")
    nx = slabs * planes

    def gray(r):
        return r + (r // 2) * (1 - 2 * (r % 2))

    def flip(pp, i):
        return i + (pp % 2) * (planes - 1 - 2 * i)

    def device_of(x):
        pair = x // (2 * planes)
        i = x % (2 * planes)
        return gray(flip(pair, i // 2)), 2 * pair + i % 2

    active = t < planes
    x = (p // 2) * 2 * planes + 2 * flip(p // 2, gray(t)) + p % 2
    home, spot = x // planes, x % planes

    def rcopy(src, dst, ss, rs, tt, pp):
        return pltpu.make_async_remote_copy(
            src_ref=src, dst_ref=dst, send_sem=ss, recv_sem=rs,
            device_id={"tm": tt, "space": pp}, device_id_type=MESH,
        )

    barrier = pltpu.get_barrier_semaphore()

    def hello(there, slab):
        pl.semaphore_signal(
            barrier, inc=1, device_id={"tm": there, "space": slab}, device_id_type=MESH
        )

    def greet(j, _):
        hello(t, (p + j) % slabs)
        return 0

    if slabs <= 16:
        for j in range(1, slabs):
            greet(j, 0)
    else:
        lax.fori_loop(1, slabs, greet, 0)
    for gap in (-1, 0, 1):
        layer = p // 2 + gap

        @pl.when(jnp.logical_and(layer >= 0, layer < slabs // 2))
        def _():
            for j in range(1, sections):
                for c in range(2):
                    hello((t + j) % sections, 2 * layer + c)

    def group(q, _):
        def slot(j, found):
            count, one, two = found
            hit = targets[p, j] == q
            one = jnp.where(jnp.logical_and(hit, count == 0), j, one)
            two = jnp.where(jnp.logical_and(hit, count == 1), j, two)
            return count + jnp.where(hit, 1, 0), one, two

        zero = jnp.int32(0)
        if slabs <= 16:
            found = (zero, zero, zero)
            for j in range(slabs):
                found = slot(j, found)
        else:
            found = lax.fori_loop(0, slabs, slot, (zero, zero, zero))
        for rank in range(2):
            line = store[pl.ds(found[1 + rank], 1), :]
            for k in range(rows):
                outgoing[q, rank, pl.ds(k, 1), :] = line[:, k * 128 : (k + 1) * 128]
        return 0

    lax.fori_loop(0, slabs, group, 0)
    for q in range(planes):
        for y in range(ny):
            for f in range(fields):
                obs[q, y, f : f + 1, :] = obs_in[f, q, y : y + 1, :]
    beside = 1 + jnp.where(p // 2 > 0, 1, 0) + jnp.where(p // 2 < slabs // 2 - 1, 1, 0)
    pl.semaphore_wait(barrier, slabs - 1 + (sections - 1) * 2 * beside)

    def a2a(peer):
        return rcopy(outgoing.at[peer], arrived.at[p], a2a_s.at[peer], a2a_r.at[p], t, peer)

    def a2a_start(j, _):
        far = slabs - j

        @pl.when(p + far < slabs)
        def _():
            a2a(p + far).start()

        @pl.when(p >= far)
        def _():
            a2a(p - far).start()

        return 0

    lax.fori_loop(1, slabs, a2a_start, 0)
    keep = pltpu.make_async_copy(outgoing.at[p], arrived.at[p], loc.at[0])
    keep.start()

    def each_obs(q, action):
        tt, pp = device_of(p * planes + q)
        same = jnp.logical_and(tt == t, pp == p)

        @pl.when(jnp.logical_not(same))
        def _():
            action(rcopy(obs.at[q], obsr.at[t], obs_s.at[q], obs_r.at[t], tt, pp), False)

        @pl.when(same)
        def _():
            action(pltpu.make_async_copy(obs.at[q], obsr.at[t], loc.at[1]), True)

    for q in range(planes):
        each_obs(q, lambda c, same: c.start())

    zeros5 = jnp.zeros((fields, 128), F32)

    taps_all = w_in.shape[1]
    weights = w_in[...]
    nt = (((1,), (1,)), ((), ()))
    for c in range(3):
        sel = jnp.where(picks((taps_all, 80), 1, 3, c, fields), 1.0, 0.0).astype(BF16)
        wf[16 * c : 16 * c + 16, :] = jnp.dot(weights, sel, preferred_element_type=F32).astype(BF16)
    for b in range(3):
        sel = jnp.where(picks((72, taps_all), 0, 1, 3 * b, fields), 1.0, 0.0).astype(BF16)
        wc[:, 16 * b : 16 * b + 16] = lax.dot_general(
            sel, weights, nt, preferred_element_type=F32
        ).astype(BF16)
    wide_out = jnp.concatenate(
        [w_out[...].astype(F32), jnp.zeros((16 - fields, 16), F32)], axis=0
    ).astype(BF16)
    wo[...] = wide_out
    eye = jnp.where(
        lax.broadcasted_iota(jnp.int32, (16, 16), 0) == lax.broadcasted_iota(jnp.int32, (16, 16), 1),
        1.0, 0.0,
    ).astype(BF16)
    wot[...] = lax.dot_general(eye, wide_out, nt, preferred_element_type=F32).astype(BF16)
    pin_ref[...] = jnp.zeros(pin_ref.shape, F32)
    pout_ref[...] = jnp.zeros(pout_ref.shape, F32)
    gpart[...] = jnp.zeros(gpart.shape, F32)

    def place(b, _):
        def holder(h, found):
            count = jnp.int32(0)
            for j in range(slabs):
                hit = targets[h, j] == p
                at = jnp.logical_and(hit, blocks[h, j] == b)
                found = jnp.where(at, 2 * h + count, found)
                count = count + jnp.where(hit, 1, 0)
            return found

        table[b] = lax.fori_loop(0, slabs, holder, jnp.int32(0))
        return 0

    if slabs <= 16:
        lax.fori_loop(0, slabs, place, 0)

    def blank(slot, recv):
        def one(i, _):
            for n in range(SEC_MOST):
                for y in range(ny):
                    stc[n, i, slot, y] = zeros5
            return 0

        lax.fori_loop(0, sections, one, 0)

        def two(i, _):
            for y in range(ny):
                recv[i, y] = zeros5
            return 0

        lax.fori_loop(0, steps, two, 0)

    @pl.when(jnp.logical_and(active, x == 0))
    def _():
        blank(0, recvm)

    @pl.when(jnp.logical_and(active, x == nx - 1))
    def _():
        blank(2, recvp)

    def a2a_wait(j, _):
        peer = (p + j) % slabs
        rcopy(outgoing.at[p], arrived.at[peer], a2a_s.at[peer], a2a_r.at[peer], t, peer).wait()
        return 0

    lax.fori_loop(1, slabs, a2a_wait, 0)
    keep.wait()

    for b in range(slabs):
        where = jnp.clip((table if slabs <= 16 else given)[b], 0, 2 * slabs - 1)
        holder = where // 2
        rank = where % 2
        for k in range(rows):
            r = b * rows + k
            f, rest = divmod(r, planes * ny)
            xx, y = divmod(rest, ny)
            full[xx, y, pl.ds(f, 1), :] = arrived[holder, rank, pl.ds(k, 1), :]

    def each_init(q, j, action):
        if (q % 2, j) in ((0, 0), (1, 2)):
            return
        xd = p * planes + q + 1 - j

        @pl.when(jnp.logical_and(xd >= 0, xd < nx))
        def _():
            tt, pp = device_of(xd)
            same = jnp.logical_and(tt == t, pp == p)

            @pl.when(jnp.logical_not(same))
            def _():
                action(
                    rcopy(full.at[q], stc.at[0, t, j], init_s.at[q, j], init_r.at[t, j], tt, pp),
                    False,
                )

            @pl.when(same)
            def _():
                action(pltpu.make_async_copy(full.at[q], stc.at[0, t, j], loc.at[2 + j]), True)

    for j in (1, 0, 2):
        for q in range(planes):
            each_init(q, j, lambda c, same: c.start())

    def finish(c, same):
        if same:
            c.wait()
        else:
            c.wait_send()

    lane = lax.broadcasted_iota(jnp.int32, (16, 128), 1)

    def up(v):
        return jnp.where(lane[: v.shape[0]] == 0, 0.0, pltpu.roll(v, 1, 1))

    def down(v):
        return jnp.where(lane[: v.shape[0]] == 127, 0.0, pltpu.roll(v, 127, 1))

    zeros3 = jnp.zeros((8 - fields, 128), F32)
    zeros8 = jnp.zeros((8, 128), F32)

    def pad8(v):
        return jnp.concatenate([v, zeros3], axis=0)

    def lanes(y):
        return slice(y * 128, (y + 1) * 128)

    t_next, p_next = device_of(x + 1)
    t_prev, p_prev = device_of(x + nx - 1 - nx * jnp.where(x > 0, 1, 0))

    def fwd(n, s, way):
        if way == 0:
            return rcopy(stc.at[n, s, 1], stc.at[n, s, 0], fwd_s.at[n - 1, s, 0],
                         fwd_r.at[n - 1, s, 0], t_next, p_next)
        return rcopy(stc.at[n, s, 1], stc.at[n, s, 2], fwd_s.at[n - 1, s, 1],
                     fwd_r.at[n - 1, s, 1], t_prev, p_prev)

    def both(make, action_next, action_prev):
        @pl.when(x < nx - 1)
        def _():
            action_next(make)

        @pl.when(x > 0)
        def _():
            action_prev(make)

    outer = 2 * (p % 2)
    partner = 2 * (p // 2) + 1 - p % 2

    def init_wait(s, j):
        xs = x - 1 + j
        ok = jnp.logical_and(xs >= 0, xs < nx)
        local_one = jnp.logical_and(s == t, (xs + planes) // planes - 1 == p)

        @pl.when(jnp.logical_and(ok, jnp.logical_not(local_one)))
        def _():
            rcopy(full.at[0], stc.at[0, s, j], init_s.at[0, 1], init_r.at[s, j], t, p).wait_recv()

        @pl.when(jnp.logical_and(ok, local_one))
        def _():
            pltpu.make_async_copy(full.at[0], stc.at[0, s, j], loc.at[2 + j]).wait()

    def pass_on(s):
        return rcopy(stc.at[0, s, 1], stc.at[0, s, outer], pair_s.at[s], pair_r.at[s], t, partner)

    def pass_in(s):
        return rcopy(stc.at[0, s, 1], stc.at[0, s, 2 - outer], pair_s.at[s], pair_r.at[s], t, partner)

    def forward(n, s):
        if n == 0:
            init_wait(s, outer)
            pass_in(s).wait_recv()
        else:
            @pl.when(x > 0)
            def _():
                fwd(n, s, 0).wait_recv()

            @pl.when(x < nx - 1)
            def _():
                fwd(n, s, 1).wait_recv()

        def row(a, y):
            if y < 0 or y >= ny:
                return zeros8
            return pad8(stc[n, s, a, y])

        for y in range(ny):
            parts = [row(a, y + b) for a in range(3) for b in (-1, 0, 1)] + [zeros8]
            taps[n, s, :, lanes(y)] = jnp.concatenate(parts, axis=0).astype(BF16)
        u_ref[0:48, :] = jnp.dot(wf[...], taps[n, s], preferred_element_type=F32)
        for y in range(ny):
            u = u_ref[16:32, lanes(y)] + up(u_ref[0:16, lanes(y)]) + down(u_ref[32:48, lanes(y)])
            h = jnp.tanh(u)
            hl[n, s, :, lanes(y)] = h.astype(BF16)
            dh[n, s, :, lanes(y)] = 1.0 - h * h
        last = n == SEC_MOST - 1
        if not last:
            c_ref[0:16, :] = jnp.dot(wo[...], hl[n, s], preferred_element_type=F32)
        for y in range(ny):
            v = row(1, y)
            xm, xp, ym, yp = row(0, y), row(2, y), row(1, y - 1), row(1, y + 1)
            zm, zp = up(v), down(v)
            dx, dy, dz = (xp - xm) * 0.5, (yp - ym) * 0.5, (zp - zm) * 0.5
            pd[n, s, y, 0] = dx * DT
            pd[n, s, y, 1] = dy * DT
            pd[n, s, y, 2] = dz * DT
            pd[n, s, y, 3] = v
            if not last:
                lap = xp + xm + yp + ym + zp + zm - 6.0 * v
                adv = v[0:1] * dx + v[1:2] * dy + v[2:3] * dz
                new = v + DT * (lap - adv) + c_ref[0:8, lanes(y)]
                stc[n + 1, s, 1, y] = new[:fields]
        if not last:
            @pl.when(x < nx - 1)
            def _():
                fwd(n + 1, s, 0).start()

            @pl.when(x > 0)
            def _():
                fwd(n + 1, s, 1).start()

    sub = lax.broadcasted_iota(jnp.int32, (8, 128), 0)

    crew = 2 * sections
    bands = slabs // 2
    part = 64 // crew
    seat = 2 * t + p % 2

    def mate(j):
        i = (seat + j) % crew
        return i, i // 2, 2 * (p // 2) + i % 2

    def red1(j):
        i, tt, pp = mate(j)
        return rcopy(gpart.at[i], g1.at[seat], r1_s.at[i], r1_r.at[seat], tt, pp)

    def red1_in(j):
        i, tt, pp = mate(j)
        return rcopy(gpart.at[i], g1.at[i], r1_s.at[i], r1_r.at[i], tt, pp)

    def red2(j):
        i = (p // 2 + j) % bands
        return rcopy(g2, g3.at[p // 2], r2_s.at[i], r2_r.at[p // 2], t, 2 * i + p % 2)

    def red2_in(j):
        i = (p // 2 + j) % bands
        return rcopy(g2, g3.at[i], r2_s.at[i], r2_r.at[i], t, 2 * i + p % 2)

    def red3(j):
        i, tt, pp = mate(j)
        return rcopy(gfin.at[seat], gfin.at[seat], r3_s.at[i], r3_r.at[seat], tt, pp)

    def red3_in(j):
        i, tt, pp = mate(j)
        return rcopy(gfin.at[i], gfin.at[i], r3_s.at[i], r3_r.at[i], tt, pp)

    def band_loop(make, action):
        def one(j, _):
            action(make(j))
            return 0

        lax.fori_loop(1, bands, one, 0)

    def red1_begin():
        for r in range(0, 64, part):
            if r < 48:
                gpart[r // part, :, 0:80] = pin_ref[r : r + part, :]
            else:
                gpart[r // part, :, 0:16] = pout_ref[r - 48 : r - 48 + part, :]
        for j in range(1, crew):
            red1(j).start()
        g1[seat] = gpart[seat]

    def chain(way, k):
        if way == 0:
            return rcopy(sendp.at[k], recvm.at[k], ch_s.at[k, 0], ch_r.at[k, 0], t_next, p_next)
        return rcopy(sendm.at[k], recvp.at[k], ch_s.at[k, 1], ch_r.at[k, 1], t_prev, p_prev)

    @pl.when(active)
    def _():
        def relay(i, _):
            s = sections - 1 - i
            init_wait(s, 1)
            pass_on(s).start()
            return 0

        lax.fori_loop(0, sections, relay, 0)
        for n in range(SEC_MOST):
            def turn(i, _):
                forward(n, sections - 1 - i)
                return 0

            lax.fori_loop(0, sections if n < SEC_MOST - 1 else 1, turn, 0)

        def obs_wait(s, _):
            same = jnp.logical_and(s == t, home == p)

            @pl.when(jnp.logical_not(same))
            def _():
                rcopy(obs.at[0], obsr.at[s], obs_s.at[0], obs_r.at[s], t, p).wait_recv()

            @pl.when(same)
            def _():
                pltpu.make_async_copy(obs.at[0], obsr.at[s], loc.at[1]).wait()

            return 0

        lax.fori_loop(0, sections, obs_wait, 0)

        blp[:, 0:128] = jnp.zeros((16, 128), BF16)
        blp[:, (ny + 1) * 128 :] = jnp.zeros((16, 128), BF16)
        for y in range(ny):
            hist[0, y] = zeros8

        size = [lengths[s] for s in range(sections)]
        after = [None] * sections
        run = jnp.int32(0)
        for s in reversed(range(sections)):
            after[s] = run
            run = run + size[s]

        def step(k, _):
            s = jnp.int32(0)
            for i in range(sections - 1):
                s = s + jnp.where(after[i] > k, 1, 0)
            n = jnp.int32(0)
            begin = jnp.int32(0)
            for i in range(sections):
                n = n + jnp.where(s == i, after[i] + size[i] - 1 - k, 0)
                begin = begin + jnp.where(s == i, after[i], 0)
            n = jnp.clip(n, 0, SEC_MOST - 1)
            first = begin == k
            weight = jnp.where(first, 1.0, 0.0).astype(F32)

            g = []
            for y in range(ny):
                v = hist[k, y] + pad8(obsr[s, y]) * weight
                g.append(v)
                gl[:, lanes(y)] = jnp.concatenate([v, zeros8], axis=0).astype(BF16)
            b32 = jnp.dot(wot[...], gl[...], preferred_element_type=F32) * dh[n, s]
            blp[:, 128 : (ny + 1) * 128] = b32.astype(BF16)
            wide = ny * 128
            stack = jnp.concatenate(
                [blp[:, 256 : 256 + wide], blp[:, 128 : 128 + wide], blp[:, 0:wide]], axis=0
            )
            c_ref[0:24, :] = jnp.dot(wc[0:24, :], stack, preferred_element_type=F32)
            c_ref[48:72, :] = jnp.dot(wc[48:72, :], stack, preferred_element_type=F32)

            def conv(a, c, y):
                return c_ref[(3 * a + c) * 8 : (3 * a + c + 1) * 8, lanes(y)]

            def speed(d, y):
                return pd[n, s, y, 3, pl.ds(d, 1), :]

            for y in range(ny):
                even = g[y] * DT
                m0 = g[y] * (0.5 * DT) * speed(0, y)
                to_next = even - m0 + conv(2, 1, y) + down(conv(2, 0, y)) + up(conv(2, 2, y))
                to_prev = even + m0 + conv(0, 1, y) + down(conv(0, 0, y)) + up(conv(0, 2, y))
                sendp[k, y] = to_next[:fields]
                sendm[k, y] = to_prev[:fields]

            @pl.when(x < nx - 1)
            def _():
                chain(0, k).start()

            @pl.when(x > 0)
            def _():
                chain(1, k).start()

            base = blp[:, 128 : 128 + wide]
            for y in range(ny):
                r = blp[:, 128 + y * 128 : 256 + y * 128].astype(F32)
                u_ref[0:16, lanes(y)] = down(r)
                u_ref[16:32, lanes(y)] = up(r)
            grads = jnp.concatenate(
                [u_ref[0:16, :].astype(BF16), base, u_ref[16:32, :].astype(BF16)], axis=0
            )
            pin_ref[...] += lax.dot_general(grads, taps[n, s], nt, preferred_element_type=F32)
            pout_ref[...] += lax.dot_general(gl[...], hl[n, s], nt, preferred_element_type=F32)

            @pl.when(k == steps - 1)
            def _():
                red1_begin()

            c_ref[24:48, :] = jnp.dot(wc[24:48, :], stack, preferred_element_type=F32)
            push, pull = [], []
            for y in range(ny):
                half = g[y] * (0.5 * DT)
                even = g[y] * DT
                m1, m2 = half * speed(1, y), half * speed(2, y)
                push.append(even - m1)
                pull.append(even + m1)
                here = g[y] * (1.0 - 6.0 * DT) + conv(1, 1, y)
                here = here + up(even - m2 + conv(1, 2, y)) + down(even + m2 + conv(1, 0, y))
                for d in range(3):
                    term = jnp.sum(g[y] * pd[n, s, y, d], axis=0, keepdims=True)
                    here = here - jnp.where(sub == d, term, 0.0)
                own[y] = here

            for y in range(ny):
                add = own[y]
                if y > 0:
                    add = add + push[y - 1]
                if y < ny - 1:
                    add = add + pull[y + 1]
                own[y] = add

            for i in range(sections - 1):
                @pl.when(k == i)
                def _():
                    forward(SEC_MOST - 1, sections - 2 - i)

            @pl.when(x > 0)
            def _():
                chain(0, k).wait_recv()

            @pl.when(x < nx - 1)
            def _():
                chain(1, k).wait_recv()

            for y in range(ny):
                hist[k + 1, y] = own[y] + pad8(recvm[k, y]) + pad8(recvp[k, y])
            return 0

        lax.fori_loop(0, steps, step, 0)

        for s in range(sections):
            at = jnp.clip(after[s] + size[s], 0, steps)
            for y in range(ny):
                osend[s, y] = hist[at, y][:fields]
        for s in range(sections):
            same = jnp.logical_and(s == t, home == p)

            @pl.when(jnp.logical_not(same))
            def _():
                rcopy(osend.at[s], out_ref.at[spot], out_s.at[s], out_r.at[spot], s, home).start()

            @pl.when(same)
            def _():
                pltpu.make_async_copy(osend.at[s], out_ref.at[spot], loc.at[5]).start()

    @pl.when(jnp.logical_not(active))
    def _():
        red1_begin()

    for j in range(1, crew):
        red1_in(j).wait()
    run1 = g1[0]
    for q in range(1, crew):
        run1 = run1 + g1[q]
    g2[...] = run1
    band_loop(red2, lambda c: c.start())
    g3[p // 2] = run1
    band_loop(red2_in, lambda c: c.wait())
    run2 = g3[0]
    for q in range(1, bands):
        run2 = run2 + g3[q]
    gfin[seat] = run2 * scale
    for j in range(1, crew):
        red3(j).start()

    for q in range(planes):
        tt, pp = device_of(p * planes + q)
        same = jnp.logical_and(tt == t, pp == p)

        @pl.when(jnp.logical_not(same))
        def _():
            rcopy(osend.at[0], out_ref.at[q], out_s.at[0], out_r.at[q], tt, pp).wait_recv()

        @pl.when(same)
        def _():
            pltpu.make_async_copy(osend.at[0], out_ref.at[q], loc.at[5]).wait()

    for q in range(planes):
        each_obs(q, lambda c, same: None if same else c.wait_send())
        for j in range(3):
            each_init(q, j, lambda c, same: None if same else c.wait_send())

    @pl.when(active)
    def _():
        def sent(s, _):
            @pl.when(jnp.logical_not(jnp.logical_and(s == t, home == p)))
            def _():
                rcopy(osend.at[s], out_ref.at[spot], out_s.at[s], out_r.at[spot], s, home).wait_send()

            pass_on(s).wait_send()
            for n in range(1, SEC_MOST):
                @pl.when(x < nx - 1)
                def _():
                    fwd(n, s, 0).wait_send()

                @pl.when(x > 0)
                def _():
                    fwd(n, s, 1).wait_send()

            return 0

        lax.fori_loop(0, sections, sent, 0)

        def sent_chain(k, _):
            @pl.when(x < nx - 1)
            def _():
                chain(0, k).wait_send()

            @pl.when(x > 0)
            def _():
                chain(1, k).wait_send()

            return 0

        lax.fori_loop(0, steps, sent_chain, 0)

    for j in range(1, crew):
        red3_in(j).wait()


def local(ckpt_store, ckpt_target, ckpt_block, lengths, obs_adjoint, w_in, w_out):
    slabs = lax.axis_size("space")
    sections = lax.axis_size("tm")
    observed = obs_adjoint[0]
    fields, planes, ny, depth = observed.shape
    block = ckpt_store.shape[3]
    rows = block // depth
    steps = 2 * sections
    channels = w_in.shape[0]
    grad_scale = 1.0 / math.sqrt(planes * slabs * ny * depth)
    vmem = pl.BlockSpec(memory_space=pltpu.VMEM)
    smem = pl.BlockSpec(memory_space=pltpu.SMEM)

    given = lengths
    if slabs > 16:
        given = pl.pallas_call(
            functools.partial(table_kernel, slabs),
            out_shape=jax.ShapeDtypeStruct((slabs,), jnp.int32),
            in_specs=[smem, smem],
            out_specs=smem,
            name="table",
        )(ckpt_target[0], ckpt_block[0])
    dims = (sections, slabs, planes, ny, fields, rows, steps, grad_scale)
    crew = 2 * sections
    part = 64 // crew
    wide = ny * depth
    face = (ny, fields, depth)
    dma = pltpu.SemaphoreType.DMA
    out, sums = pl.pallas_call(
        functools.partial(main_kernel, dims),
        out_shape=(
            jax.ShapeDtypeStruct((planes,) + face, F32),
            jax.ShapeDtypeStruct((crew, part, depth), F32),
        ),
        in_specs=[vmem, smem, smem, smem, smem, vmem, vmem, vmem],
        out_specs=(vmem, vmem),
        scratch_shapes=[
            pltpu.VMEM((slabs, 2, rows, depth), F32),
            pltpu.VMEM((planes,) + face, F32),
            pltpu.SMEM((slabs,), jnp.int32),
            pltpu.VMEM((slabs, 2, rows, depth), F32),
            pltpu.VMEM((planes,) + face, F32),
            pltpu.VMEM((SEC_MOST, sections, 3) + face, F32),
            pltpu.VMEM((sections,) + face, F32),
            pltpu.VMEM((SEC_MOST, sections, 80, wide), BF16),
            pltpu.VMEM((SEC_MOST, sections, 16, wide), F32),
            pltpu.VMEM((SEC_MOST, sections, 16, wide), BF16),
            pltpu.VMEM((SEC_MOST, sections, ny, 4, 8, depth), F32),
            pltpu.VMEM((16, wide), BF16),
            pltpu.VMEM((16, wide + 2 * depth), BF16),
            pltpu.VMEM((ny, 8, depth), F32),
            pltpu.VMEM((steps + 1, ny, 8, depth), F32),
            pltpu.VMEM((steps,) + face, F32),
            pltpu.VMEM((steps,) + face, F32),
            pltpu.VMEM((steps,) + face, F32),
            pltpu.VMEM((steps,) + face, F32),
            pltpu.VMEM((sections,) + face, F32),
            pltpu.VMEM((64, wide), F32),
            pltpu.VMEM((72, wide), F32),
            pltpu.VMEM((48, 80), BF16),
            pltpu.VMEM((72, 48), BF16),
            pltpu.VMEM((16, 16), BF16),
            pltpu.VMEM((16, 16), BF16),
            pltpu.VMEM((48, 80), F32),
            pltpu.VMEM((16, 16), F32),
            pltpu.VMEM((crew, part, depth), F32),
            pltpu.VMEM((crew, part, depth), F32),
            pltpu.VMEM((part, depth), F32),
            pltpu.VMEM((slabs // 2, part, depth), F32),
            dma((slabs,)), dma((slabs,)),
            dma((planes, 3)), dma((sections, 3)),
            dma((planes,)), dma((sections,)),
            dma((SEC_MOST - 1, sections, 2)), dma((SEC_MOST - 1, sections, 2)),
            dma((steps, 2)), dma((steps, 2)),
            dma((sections,)), dma((planes,)),
            dma((6,)),
            dma((crew,)), dma((crew,)),
            dma((slabs // 2,)), dma((slabs // 2,)),
            dma((crew,)), dma((crew,)),
            dma((sections,)), dma((sections,)),
        ],
        compiler_params=pltpu.CompilerParams(
            collective_id=0, has_side_effects=True, vmem_limit_bytes=56 * 1024 * 1024
        ),
        name="main",
    )(ckpt_store[0, 0], ckpt_target[0], ckpt_block[0], given, lengths, observed, w_in, w_out)

    start_adjoint, grad_in, grad_out = pl.pallas_call(
        finish_kernel,
        out_shape=(
            jax.ShapeDtypeStruct(observed.shape, F32),
            jax.ShapeDtypeStruct(w_in.shape, F32),
            jax.ShapeDtypeStruct(w_out.shape, F32),
        ),
        in_specs=[vmem, vmem],
        out_specs=(vmem, vmem, vmem),
        name="finish",
    )(out, sums.reshape(64, depth))
    return (start_adjoint[None], grad_in, grad_out)


def solution(mesh):
    placed = (
        P("tm", "space", None, None),
        P("tm", None, None),
        P("tm", None, None),
        P(),
        P("tm", None, "space", None, None),
        P(),
        P(),
    )
    return jax.shard_map(
        local,
        mesh=mesh,
        in_specs=placed,
        out_specs=(P("tm", None, "space", None, None), P(), P()),
        check_vma=False,
    )
```
